32 devices in a mesh: orb: 8 (over z, core), grp: 4 (over y, x).
Axes of the slice: x: 2, y: 2, z: 4, core: 2. Of those that a mesh axis runs over, the one named last changes fastest.
Arguments:
- orbitals: bfloat16 [512, 32, 1024], P('orb', 'grp'), may hold values from -6 to 6
- pair_list: int32 [8, 8, 3], replicated, may hold values from 0 to 63, as said below
- offsets: int32 [512, 3], replicated, may hold values from 0 to 15
Outputs:
- exchange_action: float32 [512, 32, 1024], P('orb', 'grp')
The draws below stay inside these ranges and needn't reach their ends.
Inputs may be any that keep to these rules, and one draw needn't show every extreme that they name: pair_list[o, r, 0] and pair_list[o, r, 1] are below 64; pair_list[o, r, 2] is a slot below 16, distinct within each block o, so a block names each owner group at most 2 times; in every draw some owner group is named 2 times by every block; the two orbitals of a pair differ.
All inputs are finite; a program needn't handle non-finite values.
Results may differ from the reference program's by a relative error of at most 0.0006.
Values may be sent and summed in bfloat16 or wider, within the bound.
A program may use at most 64 MiB of HBM per device.

```python
import math
import jax
import jax.numpy as jnp
from jax import lax

BOX = 32
ORB_GRP = 64
CAP = 2
ORBITALS = 512
N_ORB = 8


def draw_pair_list(key, part):
    slot_count = N_ORB * CAP
    keep_count = slot_count // 2
    base_key = jax.random.fold_in(key, 17)
    full_group = jax.random.randint(jax.random.fold_in(base_key, 1), (), 0, N_ORB)
    slot_ids = jnp.arange(slot_count, dtype=jnp.int32)

    def one_block(block_num):
        block_key = jax.random.fold_in(base_key, block_num + 100)
        key_score, key_second, key_first, key_other = jax.random.split(block_key, 4)
        scores = jax.random.randint(key_score, (slot_count,), 0, 1 << 20) * slot_count + slot_ids
        scores = jnp.where(slot_ids // CAP == full_group, -1 - slot_ids, scores)
        chosen = jnp.argsort(scores, stable=True)[:keep_count].astype(jnp.int32)
        second_local = jax.random.randint(key_second, (keep_count,), 0, ORB_GRP)
        first_raw = jax.random.randint(key_first, (keep_count,), 0, ORB_GRP)
        other_local = (second_local + 1 + jax.random.randint(key_other, (keep_count,), 0, ORB_GRP - 1)) % ORB_GRP
        first_local = jnp.where(chosen // CAP == block_num, other_local, first_raw)
        return jnp.stack([second_local, first_local, chosen], axis=1)
    return jax.vmap(one_block)(jnp.arange(N_ORB, dtype=jnp.int32)).astype(jnp.int32)


def with_ends(values, own_key, least, largest):
    longest = values.shape.index(max(values.shape))
    spots = []
    for shift in (0, 1):
        where = [jax.random.randint(jax.random.fold_in(own_key, axis), (), 0, length) for axis, length in enumerate(values.shape)]
        where[longest] = (where[longest] + shift) % values.shape[longest]
        spots.append(tuple(where))
    return values.at[spots[0]].set(least).at[spots[1]].set(largest)


def level_of(stream_key, shape, cuts, low, top_value):
    gain = 1.0
    for position, parts in cuts:
        draws = jax.random.uniform(jax.random.fold_in(jax.random.fold_in(stream_key, 6), position), (parts,), jnp.float32, low / len(cuts), top_value / len(cuts))
        gain = gain * jnp.repeat(jnp.exp(draws), shape[position] // parts).reshape((-1,) + (1,) * (len(shape) - 1 - position))
    return gain


def noise(own_key, extent, spread, reach, cuts=(), held_as=jnp.bfloat16):
    result = jax.random.normal(own_key, extent, jnp.float32) * spread
    if len(cuts) > 0:
        result = level_of(own_key, extent, cuts, -0.22, 0.18) * result
    return jnp.clip(result, min=-reach, max=reach).astype(held_as)


def setup_inputs(seed: int = 0) -> dict:
    key_of = jax.random.split(jax.random.key(seed), 4)
    orbitals = noise(key_of[0], (ORBITALS, BOX, BOX * BOX), 1.0, 6.0, ((0, 8), (1, 4)))
    pair_list = draw_pair_list(jax.random.fold_in(key_of[3], 71), 0)
    offsets = with_ends(jax.random.randint(key_of[2], (ORBITALS, 3), 0, BOX // 2), jax.random.fold_in(key_of[2], 1), 0, (BOX // 2) - 1).astype(jnp.int32)
    return {"orbitals": orbitals, "pair_list": pair_list, "offsets": offsets}


screen_shift = 0.25
highest = lax.Precision.HIGHEST
shared_forms = ('ab,pbyz->payz', 'ab,pxbz->pxaz', 'ab,pxyb->pxya')
single_forms = ('pab,pbyz->payz', 'pab,pxbz->pxaz', 'pab,pxyb->pxya')

def sine_table(length):
    counts = jnp.arange(length).astype(jnp.float32) + 1.0
    return jnp.sqrt(2.0 / (length + 1.0)) * jnp.sin(math.pi * counts[:, None] * counts[None, :] / (length + 1.0))

def green_table(length):
    counts = jnp.arange(length).astype(jnp.float32) + 1.0
    levels = 2.0 - 2.0 * jnp.cos(math.pi * counts / (length + 1.0))
    return 1.0 / (levels[:, None, None] + levels[None, :, None] + levels[None, None, :] + screen_shift)

def shift_tables(displace, length):
    places = jnp.arange(length, dtype=jnp.int32)
    return (places[None, None, :] == places[None, :, None] + displace[:, None, None]).astype(jnp.float32)

def along_shared(table, field, dimension):
    return jnp.einsum(shared_forms[dimension], table, field, precision=highest)

def along_single(tables, field, dimension):
    return jnp.einsum(single_forms[dimension], tables, field, precision=highest)

def pair_terms(first_box, second_box, displace):
    length = first_box.shape[1]
    transform = sine_table(length)
    tables = [shift_tables(displace[:, axis_num], length) for axis_num in range(3)]
    shifted = second_box
    for dimension in range(3):
        shifted = along_single(tables[dimension], shifted, dimension)
    charge = first_box * shifted
    for dimension in range(3):
        charge = along_shared(transform, charge, dimension)
    charge = charge * green_table(length)[None]
    for dimension in range(3):
        charge = along_shared(transform, charge, dimension)
    to_first = charge * shifted
    returned = charge * first_box
    for dimension in range(3):
        returned = along_single(jnp.swapaxes(tables[dimension], 1, 2), returned, dimension)
    return (to_first, returned)

def reference(orbitals, pair_list, offsets):
    length = orbitals.shape[1]
    groups = pair_list.shape[0]

    def accumulate(summed, block_data):
        block_pairs, block_num = block_data
        second_ids = (block_num * ORB_GRP + block_pairs[:, 0]).astype(jnp.int32)
        first_ids = (block_pairs[:, 2] // CAP * ORB_GRP + block_pairs[:, 1]).astype(jnp.int32)
        displace = (offsets[second_ids] - offsets[first_ids]).astype(jnp.int32)
        first_box = orbitals[first_ids].astype(jnp.float32).reshape(-1, length, length, length)
        second_box = orbitals[second_ids].astype(jnp.float32).reshape(-1, length, length, length)
        to_first, returned = pair_terms(first_box, second_box, displace)
        summed = summed.at[first_ids].add(to_first.reshape(-1, length, length * length))
        summed = summed.at[second_ids].add(returned.reshape(-1, length, length * length))
        return (summed, None)
    initial = jnp.zeros(orbitals.shape, jnp.float32)
    summed, unused = lax.scan(accumulate, initial, (pair_list, jnp.arange(groups, dtype=jnp.int32)))
    return summed
```

```python
import math

import jax
import jax.numpy as jnp
import ml_dtypes
import numpy as np
from jax import lax
from jax.experimental import pallas as pl
from jax.experimental.pallas import tpu as pltpu
from jax.sharding import PartitionSpec as P

BOX = 32
ORB_GRP = 64
CAP = 2


screen_shift = 0.25
F32 = jnp.float32
BF16 = jnp.bfloat16


def split_table(table):
    wide = np.asarray(table, np.float32)
    high = wide.astype(ml_dtypes.bfloat16)
    low = (wide - high.astype(np.float32)).astype(ml_dtypes.bfloat16)
    return high, low


def fixed_tables(length):
    counts = np.arange(length) + 1.0
    sine = np.sqrt(2.0 / (length + 1.0)) * np.sin(
        math.pi * counts[:, None] * counts[None, :] / (length + 1.0)
    )
    levels = 2.0 - 2.0 * np.cos(math.pi * counts / (length + 1.0))
    green = 1.0 / (
        levels[:, None, None] + levels[None, :, None] + levels[None, None, :] + screen_shift
    )
    ones = np.ones((1, length))
    return (
        np.kron(sine, ones).astype(np.float32),
        np.kron(ones, sine).astype(np.float32),
        *split_table(sine),
        green.reshape(length, length * length).astype(np.float32),
    )


def split_field(field):
    high = field.astype(BF16)
    return high, (field - high.astype(F32)).astype(BF16)


def dot(left, right):
    return jnp.dot(left, right, preferred_element_type=F32)


def pair_kernel(
    moves, boxes, outer, inner, sine_high, sine_low, green, out, shifts, fields, plane_high, plane_low
):
    length, cells = green.shape
    share = boxes.shape[0] // 2
    row = lax.broadcasted_iota(jnp.int32, (length, cells), 0)
    col = lax.broadcasted_iota(jnp.int32, (length, cells), 1)
    mid = col // length
    last = col - mid * length

    def shift(field, dx, dy, dz):
        moved = pltpu.roll(field, jnp.remainder(-dx + length, length), 0)
        flat = jnp.remainder(2 * cells - dy * length - dz, cells)
        moved = pltpu.roll(moved, flat, 1)
        x, y, z = row + dx, mid + dy, last + dz
        keep = (x >= 0) & (x < length) & (y >= 0) & (y < length) & (z >= 0) & (z < length)
        return jnp.where(keep, moved, 0.0)

    def along_plane():
        high, low = split_field(fields[...])
        fields[...] = (
            dot(high, plane_high[...]) + dot(low, plane_high[...]) + dot(high, plane_low[...])
        )

    def along_x(field):
        high, low = split_field(field)
        return dot(sine_high[...], high) + dot(sine_high[...], low) + dot(sine_low[...], high)

    @pl.loop(0, length)
    def _(step):
        rows = pl.ds(pl.multiple_of(step * length, length), length)
        plane_high[rows, :], plane_low[rows, :] = split_field(outer[pl.ds(step, 1), :] * inner[...])

    for p in range(share):
        moved = shift(boxes[share + p].astype(F32), moves[p, 0], moves[p, 1], moves[p, 2])
        shifts[p] = moved
        fields[p * length : (p + 1) * length, :] = boxes[p].astype(F32) * moved
    along_plane()
    for p in range(share):
        rows = slice(p * length, (p + 1) * length)
        fields[rows, :] = along_x(along_x(fields[rows, :]) * green[...])
    along_plane()
    for p in range(share):
        potential = fields[p * length : (p + 1) * length, :]
        out[p] = potential * shifts[p]
        out[share + p] = shift(
            potential * boxes[p].astype(F32), -moves[p, 0], -moves[p, 1], -moves[p, 2]
        )


def whole_terms(boxes, moves):
    count, length, cells = boxes.shape
    share = count // 2
    vmem = pl.BlockSpec(memory_space=pltpu.VMEM)
    return pl.pallas_call(
        pair_kernel,
        out_shape=jax.ShapeDtypeStruct((count, length, cells), F32),
        in_specs=[pl.BlockSpec(memory_space=pltpu.SMEM)] + [vmem] * 6,
        out_specs=vmem,
        scratch_shapes=[
            pltpu.VMEM((share, length, cells), F32),
            pltpu.VMEM((share * length, cells), F32),
            pltpu.VMEM((cells, cells), BF16),
            pltpu.VMEM((cells, cells), BF16),
        ],
        compiler_params=pltpu.CompilerParams(vmem_limit_bytes=48 * 1024 * 1024),
    )(moves, boxes, *[jnp.asarray(t) for t in fixed_tables(length)])


def per_device(orbitals, pair_list, offsets):
    groups = lax.axis_size("orb")
    layers = lax.axis_size("grp")
    owner_index = lax.axis_index("orb")
    region = lax.axis_index("grp")
    slab_depth = orbitals.shape[1]
    plane_cells = orbitals.shape[2]
    slot_count = groups * CAP
    cell_count = slab_depth * plane_cells
    own_pairs = lax.dynamic_index_in_dim(pair_list, owner_index, 0, keepdims=False)
    slot_ids = jnp.arange(slot_count, dtype=jnp.int32)
    send_match = own_pairs[None, :, 2] == slot_ids[:, None]
    send_valid = jnp.any(send_match, axis=1)
    source = jnp.sum(jnp.where(send_match, own_pairs[None, :, 0], 0), axis=1)
    outgoing = jnp.take(orbitals, source, axis=0) * send_valid[:, None, None].astype(jnp.bfloat16)
    incoming = lax.all_to_all(outgoing, "orb", split_axis=0, concat_axis=0, tiled=True)
    wanted = owner_index * CAP + jnp.arange(CAP, dtype=jnp.int32)
    recv_match = pair_list[:, None, :, 2] == wanted[None, :, None]
    recv_valid = jnp.any(recv_match, axis=2).reshape(slot_count)
    first_local = jnp.sum(jnp.where(recv_match, pair_list[:, None, :, 1], 0), axis=2).reshape(
        slot_count
    )
    second_local = jnp.sum(jnp.where(recv_match, pair_list[:, None, :, 0], 0), axis=2)
    second_ids = (jnp.arange(groups, dtype=jnp.int32)[:, None] * ORB_GRP + second_local).reshape(
        slot_count
    )
    first_ids = owner_index * ORB_GRP + first_local
    displace = jnp.take(offsets, second_ids, axis=0) - jnp.take(offsets, first_ids, axis=0)
    first_box = jnp.take(orbitals, first_local, axis=0)
    share_count = slot_count // layers
    by_region = (layers, share_count, slab_depth, plane_cells)
    both = jnp.concatenate([first_box.reshape(by_region), incoming.reshape(by_region)], axis=1)
    both = both.reshape(2 * slot_count, slab_depth, plane_cells)
    both_whole = lax.all_to_all(both, "grp", split_axis=0, concat_axis=1, tiled=True)
    part_moves = lax.dynamic_slice_in_dim(displace, region * share_count, share_count, 0)
    terms = whole_terms(both_whole, part_moves)
    terms = lax.all_to_all(terms, "grp", split_axis=1, concat_axis=0, tiled=True)
    terms = terms.reshape(layers, 2, share_count, slab_depth, plane_cells)
    to_first_slab = terms[:, 0].reshape(slot_count, slab_depth, plane_cells)
    returned_slab = terms[:, 1].reshape(slot_count, slab_depth, plane_cells)
    returned_home = lax.all_to_all(returned_slab, "orb", split_axis=0, concat_axis=0, tiled=True)
    local_ids = jnp.arange(orbitals.shape[0], dtype=jnp.int32)
    send_hot = (source[None, :] == local_ids[:, None]) & send_valid[None, :]
    recv_hot = (first_local[None, :] == local_ids[:, None]) & recv_valid[None, :]
    hot = jnp.concatenate([send_hot, recv_hot], axis=1).astype(BF16)
    landed = jnp.concatenate([returned_home, to_first_slab], axis=0)
    landed = landed.reshape(2 * slot_count, cell_count)
    high = lax.reduce_precision(landed, 8, 7)
    rest = landed - high
    action = dot(hot, high.astype(BF16)) + dot(hot, rest.astype(BF16))
    return action.reshape(orbitals.shape)


def solution(mesh):
    in_specs = (P("orb", "grp", None), P(), P())
    out_specs = P("orb", "grp", None)
    return jax.shard_map(
        per_device, mesh=mesh, in_specs=in_specs, out_specs=out_specs, check_vma=False
    )
```
